256 devices in a mesh: row: 16 (over x, y_lo, core), col: 16 (over y_hi, z).
Axes of the slice: x: 4, y: 4 (y_hi: 2, y_lo: 2; y = y_hi * 2 + y_lo), z: 8, core: 2. Of those that a mesh axis runs over, the one named last changes fastest.
Arguments:
- pair_state: bfloat16 [768, 768, 128], P('row', 'col'), may hold values from -6 to 6
- outgoing_norm: float32 [128], replicated, may hold values from 0.1 to 1.9
- outgoing_mixing: bfloat16 [128, 640], replicated, may hold values from -0.5 to 0.5
- outgoing_scale: float32 [128], replicated, may hold values from 0.1 to 1.9
- outgoing_final: bfloat16 [128, 128], replicated, may hold values from -0.5 to 0.5
- incoming_norm: float32 [128], replicated, may hold values from 0.1 to 1.9
- incoming_mixing: bfloat16 [128, 640], replicated, may hold values from -0.5 to 0.5
- incoming_scale: float32 [128], replicated, may hold values from 0.1 to 1.9
- incoming_final: bfloat16 [128, 128], replicated, may hold values from -0.5 to 0.5
Outputs:
- pair_out: bfloat16 [768, 768, 128], P('row', 'col')
The draws below stay inside these ranges and needn't reach their ends.
All inputs are finite; a program needn't handle non-finite values.
Results may differ from the reference program's by a relative error of at most 0.018.
Values may be sent and summed in bfloat16 or wider, within the bound.
A program may use at most 128 MiB of HBM per device.

```python
import jax
import jax.numpy as jnp
from jax import lax

C = 128
TI = 48
N = 768
TJ = 48
N_ROW = 16
N_COL = 16


def block_scale(rng, shape, split, smallest, top_value):
    level = 1.0
    for position, blocks in split:
        draws = jax.random.uniform(jax.random.fold_in(jax.random.fold_in(rng, 6), position), (blocks,), jnp.float32, smallest / len(split), top_value / len(split))
        level = level * jnp.repeat(jnp.exp(draws), shape[position] // blocks).reshape((-1,) + (1,) * (len(shape) - 1 - position))
    return level


def centred(stream_key, extent, scale, reach, split=(), held_as=jnp.bfloat16):
    drawn = scale * jax.random.normal(stream_key, extent, jnp.float32)
    if split:
        drawn = drawn * block_scale(stream_key, extent, split, -0.22, 0.18)
    return jnp.clip(drawn, -reach, reach).astype(held_as)


def setup_inputs(seed: int = 0) -> dict:
    splits = jax.random.split(jax.random.key(seed), 10)
    pair_state = centred(splits[0], (N, N, C), 1.0, 6.0, ((0, 16), (1, 16)))
    outgoing_norm = jnp.clip(1.0 + 0.18 * jax.random.normal(splits[1], (C,), jnp.float32), 0.1, 1.9)
    outgoing_mixing = centred(splits[2], (C, 5 * C), C ** -0.5, 0.5)
    outgoing_scale = jnp.clip(1.0 + 0.18 * jax.random.normal(splits[3], (C,), jnp.float32), 0.1, 1.9)
    outgoing_final = centred(splits[4], (C, C), C ** -0.5, 0.5)
    incoming_norm = jnp.clip(1.0 + 0.18 * jax.random.normal(splits[5], (C,), jnp.float32), 0.1, 1.9)
    incoming_mixing = centred(splits[6], (C, 5 * C), C ** -0.5, 0.5)
    incoming_scale = jnp.clip(1.0 + 0.18 * jax.random.normal(splits[7], (C,), jnp.float32), 0.1, 1.9)
    incoming_final = centred(splits[8], (C, C), C ** -0.5, 0.5)
    return {"pair_state": pair_state, "outgoing_norm": outgoing_norm, "outgoing_mixing": outgoing_mixing, "outgoing_scale": outgoing_scale, "outgoing_final": outgoing_final, "incoming_norm": incoming_norm, "incoming_mixing": incoming_mixing, "incoming_scale": incoming_scale, "incoming_final": incoming_final}


def normalize(values, channel_gain):
    floated = values.astype(jnp.float32)
    center = lax.optimization_barrier(jnp.mean(floated, axis=-1, keepdims=True))
    spread = lax.optimization_barrier(jnp.mean((floated - center) ** 2, axis=-1, keepdims=True))
    return ((floated - center) * lax.rsqrt(spread + 1e-05) * channel_gain).astype(jnp.bfloat16)

def gated_product(normed, weights, column):
    width = weights.shape[0]
    flat = normed.reshape(-1, width)
    gating = jnp.dot(flat, weights[:, column * width:(column + 1) * width], preferred_element_type=jnp.float32)
    content = jnp.dot(flat, weights[:, (column + 1) * width:(column + 2) * width], preferred_element_type=jnp.float32)
    return (jax.nn.sigmoid(gating) * content).astype(jnp.bfloat16).reshape(normed.shape)

def finish_update(pair_field, normed, product, weights, scale, final):
    width = weights.shape[0]
    mixed = normalize(product, scale)
    gating = jax.nn.sigmoid(jnp.dot(normed.reshape(-1, width), weights[:, 4 * width:], preferred_element_type=jnp.float32))
    update = gating * jnp.dot(mixed.reshape(-1, width), final, preferred_element_type=jnp.float32)
    return (pair_field.astype(jnp.float32) + update.reshape(pair_field.shape)).astype(jnp.bfloat16)

def half_update(pair_field, norm_gain, weights, scale, final, outgoing):
    normed = normalize(pair_field, norm_gain)
    first_factor = gated_product(normed, weights, 0)
    second_factor = gated_product(normed, weights, 2)
    if outgoing:
        block_width, block_count, axis_index, formula = (TJ, N_COL, 1, 'ikc,jkc->ijc')
    else:
        block_width, block_count, axis_index, formula = (TI, N_ROW, 0, 'kic,kjc->ijc')

    def accumulate(carry, block_index):
        offset = (block_index * block_width).astype(jnp.int32)
        first_block = lax.dynamic_slice_in_dim(first_factor, offset, block_width, axis_index).astype(jnp.float32)
        second_block = lax.dynamic_slice_in_dim(second_factor, offset, block_width, axis_index).astype(jnp.float32)
        partial_sum = jnp.einsum(formula, first_block, second_block)
        rounded = lax.optimization_barrier(partial_sum.astype(jnp.bfloat16))
        return (carry + rounded.astype(jnp.float32), None)
    initial = jnp.zeros(pair_field.shape, jnp.float32)
    product, unused = lax.scan(accumulate, initial, jnp.arange(block_count, dtype=jnp.int32))
    return finish_update(pair_field, normed, product, weights, scale, final)

def reference(pair_state, outgoing_norm, outgoing_mixing, outgoing_scale, outgoing_final, incoming_norm, incoming_mixing, incoming_scale, incoming_final):
    middle = half_update(pair_state, outgoing_norm, outgoing_mixing, outgoing_scale, outgoing_final, True)
    return half_update(middle, incoming_norm, incoming_mixing, incoming_scale, incoming_final, False)
```

```python
import functools

import jax
import jax.numpy as jnp
from jax import lax
from jax.experimental import pallas as pl
from jax.experimental.pallas import tpu as pltpu
from jax.sharding import PartitionSpec as P

MESH = pl.DeviceIdType.MESH


def exchange_kernel(axis, n, x_ref, o_ref, send, recv, local):
    me = lax.axis_index(axis)
    barrier = pltpu.get_barrier_semaphore()

    def greet(s, carry):
        pl.semaphore_signal(
            barrier, inc=1, device_id={axis: lax.rem(me + s, n)}, device_id_type=MESH
        )
        return carry

    def copy(p, slot):
        return pltpu.make_async_remote_copy(
            src_ref=x_ref.at[p],
            dst_ref=o_ref.at[slot],
            send_sem=send.at[p],
            recv_sem=recv.at[slot],
            device_id={axis: p},
            device_id_type=MESH,
        )

    def start(s, carry):
        copy(lax.rem(me + s, n), me).start()
        return carry

    def finish(s, carry):
        p = lax.rem(me + s, n)
        landed = copy(p, p)
        landed.wait_recv()
        landed.wait_send()
        return carry

    lax.fori_loop(1, n, greet, 0)
    own = pltpu.make_async_copy(x_ref.at[me], o_ref.at[me], local)
    own.start()
    pl.semaphore_wait(barrier, n - 1)
    lax.fori_loop(1, n, start, 0)
    lax.fori_loop(1, n, finish, 0)
    own.wait()


def exchange(x, axis, call_id):
    n = x.shape[0]
    return pl.pallas_call(
        functools.partial(exchange_kernel, axis, n),
        out_shape=jax.ShapeDtypeStruct(x.shape, x.dtype),
        in_specs=[pl.BlockSpec(memory_space=pl.ANY)],
        out_specs=pl.BlockSpec(memory_space=pl.ANY),
        scratch_shapes=[
            pltpu.SemaphoreType.DMA((n,)),
            pltpu.SemaphoreType.DMA((n,)),
            pltpu.SemaphoreType.DMA,
        ],
        name=f"exchange_{axis}_{call_id}",
        compiler_params=pltpu.CompilerParams(collective_id=call_id, has_side_effects=True),
    )(x)


def normalize(values, gain, axis=-1):
    floated = values.astype(jnp.float32)
    center = jnp.mean(floated, axis=axis, keepdims=True)
    spread = jnp.mean((floated - center) ** 2, axis=axis, keepdims=True)
    return ((floated - center) * lax.rsqrt(spread + 1e-05) * gain).astype(jnp.bfloat16)


def update(field, gain, weights, scale, final, outgoing, ids):
    rows, cols, c = field.shape
    n_row, n_col = lax.axis_size("row"), lax.axis_size("col")
    per = c // n_col
    normed = normalize(field, gain).reshape(rows * cols, c)

    def turned(column):
        return lax.dot_general(
            weights[:, column * c : (column + 1) * c],
            normed,
            (((0,), (1,)), ((), ())),
            preferred_element_type=jnp.float32,
        )

    first = (jax.nn.sigmoid(turned(0)) * turned(1)).astype(jnp.bfloat16)
    second = (jax.nn.sigmoid(turned(2)) * turned(3)).astype(jnp.bfloat16)
    packed = jnp.concatenate(
        [first.reshape(n_col, per, -1), second.reshape(n_col, per, -1)], axis=1
    )
    swapped = exchange(packed, "col", ids)
    wide = (
        swapped.reshape(n_col, 2 * per, rows, cols)
        .transpose(1, 2, 0, 3)
        .reshape(2, per, rows, n_col * cols)
    )
    left, right = wide[0], wide[1]
    if outgoing:
        left = left.reshape(per * 2, rows // 2, n_col * cols)
        right = jnp.repeat(right, 2, axis=0)
        cut = rows // 2
        got = exchange(jnp.concatenate([left, right], axis=1), "row", ids + 1)
        lhs = got[:, :cut].reshape(-1, n_col * cols)
        rhs = got[:, cut:].reshape(-1, n_col * cols)
        product = lax.dot_general(
            lhs, rhs, (((1,), (1,)), ((), ())), preferred_element_type=jnp.float32
        ).astype(jnp.bfloat16)
        back = exchange(product.reshape(n_row, cut, n_col * cols), "row", ids + 2)
        back = back.reshape(per, rows, n_col, cols)
    else:
        half = n_col * cols // 2
        left = jnp.repeat(left, 2, axis=0)
        right = right.reshape(per, rows, 2, half).transpose(0, 2, 1, 3)
        right = right.reshape(per * 2, rows, half)
        got = exchange(jnp.concatenate([left, right], axis=2), "row", ids + 1)
        got = got.reshape(-1, 3 * half)
        product = lax.dot_general(
            got[:, : 2 * half],
            got[:, 2 * half :],
            (((0,), (0,)), ((), ())),
            preferred_element_type=jnp.float32,
        ).astype(jnp.bfloat16)
        back = exchange(product.reshape(n_row, rows, half), "row", ids + 2)
        back = back.reshape(per, 2, rows, half).transpose(0, 2, 1, 3)
        back = back.reshape(per, rows, n_col, cols)
    parts = back.transpose(2, 0, 1, 3).reshape(n_col, per, rows * cols)
    product = exchange(parts, "col", ids + 3).reshape(c, rows * cols)
    mixed = normalize(product, scale[:, None], axis=0)
    gating = jax.nn.sigmoid(
        jnp.dot(normed, weights[:, 4 * c :], preferred_element_type=jnp.float32)
    )
    change = gating * lax.dot_general(
        mixed, final, (((0,), (0,)), ((), ())), preferred_element_type=jnp.float32
    )
    return (field.astype(jnp.float32) + change.reshape(field.shape)).astype(jnp.bfloat16)


def body(state, n1, m1, s1, f1, n2, m2, s2, f2):
    middle = update(state, n1, m1, s1, f1, True, 1)
    return update(middle, n2, m2, s2, f2, False, 5)


def solution(mesh):
    placed = (P("row", "col", None), P(), P(), P(), P(), P(), P(), P(), P())
    return jax.shard_map(
        body, mesh=mesh, in_specs=placed, out_specs=P("row", "col", None), check_vma=False
    )
```

```python
import functools

import jax
import jax.numpy as jnp
from jax import lax
from jax.experimental import pallas as pl
from jax.experimental.pallas import tpu as pltpu
from jax.sharding import PartitionSpec as P

MESH = pl.DeviceIdType.MESH
N_ROW, N_COL, T, C = 16, 16, 48, 128
PER = C // N_COL
N = N_ROW * T
IH, TH = T // 8, T // 16
LANES = TH * 128
F32, BF16 = jnp.float32, jnp.bfloat16
NT = (((1,), (1,)), ((), ()))
TN = (((0,), (0,)), ((), ()))


def normalize(x, axis):
    center = jnp.mean(x, axis=axis, keepdims=True)
    spread = jnp.mean((x - center) ** 2, axis=axis, keepdims=True)
    return (x - center) * lax.rsqrt(spread + 1e-05)


def block_transpose(v):
    block = lax.broadcasted_iota(jnp.int32, v[0].shape, 1) // 16
    for step in (1, 2, 4):
        low = (block & step) == 0
        out = list(v)
        for a in range(8):
            if a & step == 0:
                x, y = v[a], v[a + step]
                out[a] = jnp.where(low, x, pltpu.roll(y, 16 * step, 1))
                out[a + step] = jnp.where(low, pltpu.roll(x, 128 - 16 * step, 1), y)
        v = out
    return v


def kernel(
    outgoing,
    z_ref, gain_ref, w_ref, scale_ref, final_ref,
    out_ref,
    wt, normed, gate, scale_t,
    send1, got1, wide, send2, left, right, send3, got3, wide3, send4, got4,
    s1, r1, s2a, r2a, s2b, r2b, sf, s3, r3, s4, r4, local,
):
    row, col = lax.axis_index("row"), lax.axis_index("col")
    chan, half = row // 2, row % 2
    barrier = pltpu.get_barrier_semaphore()

    def each(first, last, body):
        def step(s, carry):
            body(s)
            return carry

        lax.fori_loop(first, last, step, 0)

    def greet(s):
        pl.semaphore_signal(
            barrier, inc=1, device_id={"row": lax.rem(row + s, N_ROW)}, device_id_type=MESH
        )
        pl.semaphore_signal(
            barrier, inc=1, device_id={"col": lax.rem(col + s, N_COL)}, device_id_type=MESH
        )

    each(1, 16, greet)

    def remote(src, dst, send, recv, axis, peer):
        return pltpu.make_async_remote_copy(
            src_ref=src, dst_ref=dst, send_sem=send, recv_sem=recv,
            device_id={axis: peer}, device_id_type=MESH,
        )

    wt[...] = jnp.transpose(w_ref[...].astype(F32)).astype(BF16)
    scale_t[...] = jnp.transpose(jnp.broadcast_to(scale_ref[...], (C, C)))

    def project(array, ih):
        x = normed[pl.ds(pl.multiple_of(ih * LANES, LANES), LANES), :]
        base = 2 * C * array
        g = lax.dot_general(wt[base : base + C, :], x, NT, preferred_element_type=F32)
        v = lax.dot_general(wt[base + C : base + 2 * C, :], x, NT, preferred_element_type=F32)
        made = jax.nn.sigmoid(g) * v
        send1[array, :, pl.ds(ih, 1)] = made.reshape(N_COL, 1, PER, LANES).astype(BF16)

    def prepare(ih):
        lines = pl.ds(pl.multiple_of(ih * 8, 8), 8)
        x = jnp.concatenate(
            [z_ref[lines, 16 * t : 16 * t + 16, :].reshape(128, C) for t in range(TH)], axis=0
        ).astype(F32)
        x = (normalize(x, 1) * gain_ref[...]).astype(BF16)
        normed[pl.ds(pl.multiple_of(ih * LANES, LANES), LANES), :] = x
        project(0, ih)

    each(0, IH, prepare)

    def col1(array, peer, slot):
        return remote(
            send1.at[array, peer], got1.at[array, slot],
            s1.at[array, peer], r1.at[array, slot], "col", peer,
        )

    def own1(array):
        return pltpu.make_async_copy(
            send1.at[array, col], got1.at[array, col], local.at[array]
        )

    pl.semaphore_wait(barrier, 30)
    each(1, N_COL, lambda s: col1(0, lax.rem(col + s, N_COL), col).start())
    own1(0).start()
    each(0, IH, lambda ih: project(1, ih))
    each(1, N_COL, lambda s: col1(1, lax.rem(col + s, N_COL), col).start())
    own1(1).start()

    def gating(ih):
        lines = pl.ds(pl.multiple_of(ih * LANES, LANES), LANES)
        gate[lines, :] = jax.nn.sigmoid(
            jnp.dot(normed[lines, :], w_ref[:, 4 * C :], preferred_element_type=F32)
        )

    each(0, IH, gating)

    def widen(array):
        def landed(s):
            peer = lax.rem(col + s, N_COL)
            col1(array, peer, peer).wait_recv()

        each(1, N_COL, landed)
        own1(array).wait()
        for u in range(2):
            for t in range(TH):
                v = [
                    got1[array, 8 * u + q, :, :, 128 * t : 128 * t + 128]
                    .astype(F32)
                    .reshape(IH * PER, 128)
                    for q in range(8)
                ]
                tile = u * TH + t
                for il, w in enumerate(block_transpose(v)):
                    for ih in range(IH):
                        wide[tile, ih * 64 + il * 8 : ih * 64 + il * 8 + 8] = w[
                            ih * 8 : ih * 8 + 8
                        ]

        for c in range(PER):
            for tile in range(2 * TH):
                send2[array, c, :, :, 128 * tile : 128 * tile + 128] = (
                    wide[tile, pl.ds(c, T, stride=8), :].astype(BF16).reshape(TH, 16, 128)
                )

    def place(ref, source):
        return ref.at[source // 8, :, lax.rem(source, 8)]

    if outgoing:
        sources_a, upper = 8, row // 8

        def pair_a(c, source):
            return send2.at[0, c], left.at[lax.rem(source, 8)], 2 * c + source // 8

    else:
        sources_a, upper = 16, 0

        def pair_a(s, source):
            c, h = s // 2, lax.rem(s, 2)
            cut = pl.ds(pl.multiple_of(h * LANES, LANES), LANES)
            return send2.at[0, c, :, :, cut], place(left, source), s

    def send_a(s):
        src, dst, peer = pair_a(s, row)

        @pl.when(peer != row)
        def _():
            remote(src, dst, s2a.at[s], r2a.at[row], "row", peer).start()

        @pl.when(peer == row)
        def _():
            pltpu.make_async_copy(src, dst, r2a.at[row]).start()

    def sent_a(s):
        src, dst, peer = pair_a(s, row)

        @pl.when(peer != row)
        def _():
            remote(src, dst, s2a.at[s], r2a.at[row], "row", peer).wait_send()

    def take_a(s):
        source = half * 8 + s if outgoing else s
        src, dst, peer = pair_a(0, source)

        @pl.when(source != row)
        def _():
            remote(src, dst, s2a.at[0], r2a.at[source], "row", source).wait_recv()

        @pl.when(source == row)
        def _():
            pltpu.make_async_copy(src, dst, r2a.at[source]).wait()

    widen(0)
    each(0, sources_a, send_a)

    def copy_b(c, source, peer):
        return remote(
            send2.at[1, c], place(right, source), s2b.at[c], r2b.at[source], "row", peer
        )

    def own_b():
        return pltpu.make_async_copy(send2.at[1, chan], place(right, row), r2b.at[row])

    partner = chan * 2 + (1 - half)

    def hand(source):
        return remote(
            place(right, source), place(right, source), sf.at[source], r2b.at[source],
            "row", partner,
        )

    def send_b(s):
        c = lax.rem(chan + s, PER)
        copy_b(c, row, 2 * c + half).start()

    widen(1)
    own_b().start()
    each(1, PER, send_b)
    each(0, sources_a, take_a)

    def pass_on(s):
        c = lax.rem(chan + s, PER)
        source = 2 * c + half
        copy_b(c, source, source).wait_recv()
        hand(source).start()

    own_b().wait()
    hand(row).start()
    each(1, PER, pass_on)

    def take_b(c):
        source = 2 * c + (1 - half)
        hand(source).wait_recv()

    each(0, PER, take_b)

    def copy3(m, s, peer, slot):
        return remote(
            send3.at[m, s], got3.at[m, slot], s3.at[m, s], r3.at[m, slot], "row", peer
        )

    def own3(m):
        return pltpu.make_async_copy(
            send3.at[m, lax.rem(row, 8)], got3.at[m, chan], r3.at[m, chan]
        )

    mine = row // 8 == half
    for m in range(TH):
        if outgoing:
            made = lax.dot_general(
                left[:, m].reshape(128, N), right[...].reshape(N, N), NT,
                preferred_element_type=F32,
            )
        else:
            made = lax.dot_general(
                left[:, :, :, :, 128 * m : 128 * m + 128].reshape(N, 128),
                right[...].reshape(N, N), TN, preferred_element_type=F32,
            )
        send3[m] = made.astype(BF16).reshape(8, 16, N)

        def send_p(s):
            peer = half * 8 + s

            @pl.when(peer != row)
            def _():
                copy3(m, s, peer, chan).start()

        each(0, 8, send_p)

        @pl.when(mine)
        def _():
            own3(m).start()

    def col4(m, peer, slot):
        return remote(
            send4.at[peer, pl.ds(2 * m, 2)], got4.at[slot, pl.ds(2 * m, 2)],
            s4.at[m, peer], r4.at[m, slot], "col", peer,
        )

    def own4(m):
        return pltpu.make_async_copy(
            send4.at[col, pl.ds(2 * m, 2)], got4.at[col, pl.ds(2 * m, 2)], local.at[2 + m]
        )

    for m in range(TH):

        def take_p(c):
            source = 2 * c + row // 8

            @pl.when(source != row)
            def _():
                copy3(m, 0, source, c).wait_recv()

            @pl.when(source == row)
            def _():
                own3(m).wait()

        each(0, PER, take_p)
        for c in range(PER):
            for tile in range(2 * TH):
                wide3[tile, pl.ds(c, 16, stride=8), :] = got3[
                    m, c, :, 128 * tile : 128 * tile + 128
                ].astype(F32)
        for u in range(2):
            for t in range(TH):
                tile = u * TH + t
                v = [
                    jnp.concatenate(
                        [
                            wide3[tile, ih * 64 + il * 8 : ih * 64 + il * 8 + 8]
                            for ih in range(2)
                        ],
                        axis=0,
                    )
                    for il in range(8)
                ]
                for q, w in enumerate(block_transpose(v)):
                    send4[8 * u + q, 2 * m : 2 * m + 2, :, 128 * t : 128 * t + 128] = w.reshape(
                        2, PER, 128
                    ).astype(BF16)
        each(1, N_COL, lambda s: col4(m, lax.rem(col + s, N_COL), col).start())
        own4(m).start()

    for m in range(TH):

        def landed4(s):
            peer = lax.rem(col + s, N_COL)
            col4(m, peer, peer).wait_recv()

        each(1, N_COL, landed4)
        own4(m).wait()

        def finish(ih):
            lines = pl.ds(pl.multiple_of(ih * 8, 8), 8)
            x = got4[:, pl.ds(ih, 1)].astype(F32).reshape(C, LANES)
            x = normalize(x, 0) * jnp.concatenate([scale_t[...]] * TH, axis=1)
            change = lax.dot_general(
                x.astype(BF16), final_ref[...], TN, preferred_element_type=F32
            )
            change = change * gate[pl.ds(pl.multiple_of(ih * LANES, LANES), LANES), :]
            for t in range(TH):
                there = z_ref[lines, 16 * t : 16 * t + 16, :].astype(F32)
                there = there + change[128 * t : 128 * t + 128].reshape(8, 16, C)
                out_ref[lines, 16 * t : 16 * t + 16, :] = there.astype(BF16)

        each(2 * m, 2 * m + 2, finish)

    for array in range(2):
        each(
            1, N_COL,
            lambda s: col1(array, lax.rem(col + s, N_COL), col).wait_send(),
        )
    each(0, sources_a, sent_a)
    each(1, PER, lambda s: copy_b(lax.rem(chan + s, PER), row, row).wait_send())
    each(0, PER, lambda c: hand(2 * c + half).wait_send())
    for m in range(TH):

        def sent_p(s):
            peer = half * 8 + s

            @pl.when(peer != row)
            def _():
                copy3(m, s, peer, chan).wait_send()

        each(0, 8, sent_p)
        each(1, N_COL, lambda s: col4(m, lax.rem(col + s, N_COL), col).wait_send())


def update(field, gain, weights, scale, final, outgoing, call_id):
    vm = pltpu.VMEM
    dma = pltpu.SemaphoreType.DMA
    left = (8, TH, 16, N) if outgoing else (2, TH, 8, 16, LANES)
    return pl.pallas_call(
        functools.partial(kernel, outgoing),
        out_shape=jax.ShapeDtypeStruct(field.shape, field.dtype),
        scratch_shapes=[
            vm((5 * C, C), BF16),
            vm((T * T, C), BF16),
            vm((T * T, C), F32),
            vm((C, C), F32),
            vm((2, N_COL, IH, PER, LANES), BF16),
            vm((2, N_COL, IH, PER, LANES), BF16),
            vm((2 * TH, T * PER, 128), F32),
            vm((2, PER, TH, 16, N), BF16),
            vm(left, BF16),
            vm((2, TH, 8, 16, N), BF16),
            vm((TH, 8, 16, N), BF16),
            vm((TH, PER, 16, N), BF16),
            vm((2 * TH, 16 * PER, 128), F32),
            vm((N_COL, IH, PER, LANES), BF16),
            vm((N_COL, IH, PER, LANES), BF16),
            dma((2, N_COL)), dma((2, N_COL)),
            dma((N_ROW,)), dma((N_ROW,)),
            dma((PER,)), dma((N_ROW,)), dma((N_ROW,)),
            dma((TH, 8)), dma((TH, PER)),
            dma((TH, N_COL)), dma((TH, N_COL)),
            dma((2 + TH,)),
        ],
        name="outgoing" if outgoing else "incoming",
        compiler_params=pltpu.CompilerParams(collective_id=call_id, has_side_effects=True),
    )(field, gain.reshape(1, C), weights, scale.reshape(1, C), final)


def body(state, n1, m1, s1, f1, n2, m2, s2, f2):
    middle = update(state, n1, m1, s1, f1, True, 1)
    return update(middle, n2, m2, s2, f2, False, 2)


def solution(mesh):
    placed = (P("row", "col", None), P(), P(), P(), P(), P(), P(), P(), P())
    return jax.shard_map(
        body, mesh=mesh, in_specs=placed, out_specs=P("row", "col", None), check_vma=False
    )
```

```python
import jax
import jax.numpy as jnp
from jax import lax
from jax.experimental import pallas as pl
from jax.experimental.pallas import tpu as pltpu
from jax.sharding import PartitionSpec as P

MESH = pl.DeviceIdType.MESH
N_ROW, N_COL, T, C = 16, 16, 48, 128
PER = C // N_COL
N = N_ROW * T
IH, TH = T // 8, T // 16
LANES = TH * 128
F32, BF16 = jnp.float32, jnp.bfloat16
NT = (((1,), (1,)), ((), ()))
TN = (((0,), (0,)), ((), ()))


def normalize(x, axis):
    center = jnp.mean(x, axis=axis, keepdims=True)
    spread = jnp.mean((x - center) ** 2, axis=axis, keepdims=True)
    return (x - center) * lax.rsqrt(spread + 1e-05)


def block_transpose(v):
    block = lax.broadcasted_iota(jnp.int32, v[0].shape, 1) // 16
    for step in (1, 2, 4):
        low = (block & step) == 0
        out = list(v)
        for a in range(8):
            if a & step == 0:
                x, y = v[a], v[a + step]
                out[a] = jnp.where(low, x, pltpu.roll(y, 16 * step, 1))
                out[a + step] = jnp.where(low, pltpu.roll(x, 128 - 16 * step, 1), y)
        v = out
    return v


def each(first, last, body):
    def step(s, carry):
        body(s)
        return carry

    lax.fori_loop(first, last, step, 0)


def lines_of(ih):
    return pl.ds(pl.multiple_of(ih * LANES, LANES), LANES)


def remote(src, dst, send, recv, axis, peer):
    return pltpu.make_async_remote_copy(
        src_ref=src, dst_ref=dst, send_sem=send, recv_sem=recv,
        device_id={axis: peer}, device_id_type=MESH,
    )


BUFFERS = (
    "wt", "normed", "gate", "scale_t", "field",
    "send_b", "got_b", "send_a", "got_a",
    "row_b", "right", "row_a", "left", "send_p", "got_p", "send_o", "got_o",
    "sb1", "rb1", "sa1", "ra1", "sb2", "rb2", "sf", "sa2", "ra2",
    "s3", "r3", "s4", "r4", "local",
)


def buffers(outgoing):
    vm, dma = pltpu.VMEM, pltpu.SemaphoreType.DMA
    rows = (TH, N_COL, 2, PER, LANES)
    first = rows if outgoing else (TH, N_COL, IH, PER, 128)
    return [
        vm((5 * C, C), BF16), vm((T * T, C), BF16), vm((T * T, C), F32), vm((C, C), F32),
        vm((T * T, C), BF16),
        vm(rows, BF16), vm(rows, BF16), vm(first, BF16), vm(first, BF16),
        vm((TH, PER, 16, N), BF16), vm((2, TH, 8, 16, N), BF16),
        vm((TH, PER, 16, N) if outgoing else (TH, PER, 2, TH, 16, 128), BF16),
        vm((TH, 8, 16, N) if outgoing else (TH, 2, TH, 8, 16, 128), BF16),
        vm((TH, 8, 16, N), BF16), vm((TH, PER, 16, N), BF16),
        vm(rows, BF16), vm(rows, BF16),
        dma((TH, N_COL)), dma((TH, N_COL)), dma((TH, N_COL)), dma((TH, N_COL)),
        dma((TH, PER)), dma((TH, N_ROW)), dma((TH, PER)),
        dma((TH, N_ROW)), dma((TH, N_ROW)),
        dma((TH, 8)), dma((TH, PER)),
        dma((TH, N_COL)), dma((TH, N_COL)),
        dma((3, TH)),
    ]


class Update:
    def __init__(self, outgoing, wide, gain, weights, scale, final, refs):
        self.outgoing, self.wide = outgoing, wide
        self.gain, self.weights, self.scale, self.final = gain, weights, scale, final
        self.__dict__.update(zip(BUFFERS, refs))
        self.row, self.col = lax.axis_index("row"), lax.axis_index("col")
        self.chan, self.half = self.row // 2, self.row % 2

    def ready(self):
        self.wt[...] = jnp.transpose(self.weights[...].astype(F32)).astype(BF16)
        self.scale_t[...] = jnp.transpose(jnp.broadcast_to(self.scale[...], (C, C)))

    def prepare(self, ih):
        x = self.field[lines_of(ih), :].astype(F32)
        self.normed[lines_of(ih), :] = (normalize(x, 1) * self.gain[...]).astype(BF16)

    def project(self, array, ih):
        x, base = self.normed[lines_of(ih), :], 2 * C * array
        g = lax.dot_general(self.wt[base : base + C, :], x, NT, preferred_element_type=F32)
        v = lax.dot_general(
            self.wt[base + C : base + 2 * C, :], x, NT, preferred_element_type=F32
        )
        return jax.nn.sigmoid(g) * v

    def make_b(self, m):
        for e in range(2):
            made = self.project(1, 2 * m + e)
            self.send_b[m, :, e] = made.reshape(N_COL, PER, LANES).astype(BF16)

    def make_a(self, m):
        for e in range(2):
            made = self.project(0, 2 * m + e)
            if self.outgoing:
                self.send_a[m, :, e] = made.reshape(N_COL, PER, LANES).astype(BF16)
            else:
                for t in range(TH):
                    piece = made[:, 128 * t : 128 * t + 128].reshape(N_COL, PER, 128)
                    self.send_a[t, :, 2 * m + e] = piece.astype(BF16)

    def gating(self, ih):
        self.gate[lines_of(ih), :] = jax.nn.sigmoid(
            jnp.dot(
                self.normed[lines_of(ih), :], self.weights[:, 4 * C :],
                preferred_element_type=F32,
            )
        )

    def col_copy(self, sets, m, peer, slot):
        src, dst, send, recv, _ = sets
        return remote(
            src.at[m, peer], dst.at[m, slot], send.at[m, peer], recv.at[m, slot], "col", peer
        )

    def col_own(self, sets, m):
        src, dst, _, _, k = sets
        return pltpu.make_async_copy(
            src.at[m, self.col], dst.at[m, self.col], self.local.at[k, m]
        )

    def col_start(self, sets, m):
        each(
            1, N_COL,
            lambda s: self.col_copy(sets, m, lax.rem(self.col + s, N_COL), self.col).start(),
        )
        self.col_own(sets, m).start()

    def col_take(self, sets, m):
        def landed(s):
            peer = lax.rem(self.col + s, N_COL)
            self.col_copy(sets, m, peer, peer).wait_recv()

        each(1, N_COL, landed)
        self.col_own(sets, m).wait()

    def col_sent(self, sets, m):
        each(
            1, N_COL,
            lambda s: self.col_copy(
                sets, m, lax.rem(self.col + s, N_COL), self.col
            ).wait_send(),
        )

    @property
    def set_b(self):
        return self.send_b, self.got_b, self.sb1, self.rb1, 0

    @property
    def set_a(self):
        return self.send_a, self.got_a, self.sa1, self.ra1, 1

    @property
    def set_o(self):
        return self.send_o, self.got_o, self.s4, self.r4, 2

    def widen_rows(self, got, out, m):
        def side(u):
            for t in range(TH):
                v = [
                    got[m, 8 * u + q, :, :, 128 * t : 128 * t + 128]
                    .astype(F32)
                    .reshape(2 * PER, 128)
                    for q in range(8)
                ]
                for il, w in enumerate(block_transpose(v)):
                    for e in range(2):
                        self.wide[
                            u * TH + t, e * 64 + il * 8 : e * 64 + il * 8 + 8
                        ] = w[e * 8 : e * 8 + 8]

        each(0, 2, side)
        for c in range(PER):
            for tile in range(2 * TH):
                out[m, c, :, 128 * tile : 128 * tile + 128] = self.wide[
                    tile, pl.ds(c, 16, stride=8), :
                ].astype(BF16)

    def widen_lanes(self, got, out, t):
        def side(u):
            v = [
                got[t, 8 * u + q].astype(F32).reshape(IH * PER, 128) for q in range(8)
            ]
            for il, w in enumerate(block_transpose(v)):
                for ih in range(IH):
                    third, e = ih // 2, ih % 2
                    self.wide[
                        u * TH + third, e * 64 + il * 8 : e * 64 + il * 8 + 8
                    ] = w[ih * 8 : ih * 8 + 8]

        each(0, 2, side)
        for c in range(PER):
            for u in range(2):
                for third in range(TH):
                    out[t, c, u, third] = self.wide[
                        u * TH + third, pl.ds(c, 16, stride=8), :
                    ].astype(BF16)

    def place_b(self, m, source):
        return self.right.at[source // 8, m, lax.rem(source, 8)]

    def copy_b(self, m, c, source, peer):
        return remote(
            self.row_b.at[m, c], self.place_b(m, source), self.sb2.at[m, c],
            self.rb2.at[m, source], "row", peer,
        )

    def own_b(self, m):
        return pltpu.make_async_copy(
            self.row_b.at[m, self.chan], self.place_b(m, self.row), self.rb2.at[m, self.row]
        )

    def hand(self, m, source):
        there = self.place_b(m, source)
        return remote(
            there, there, self.sf.at[m, source // 2], self.rb2.at[m, source], "row",
            self.chan * 2 + (1 - self.half),
        )

    def spread_b(self, m):
        self.col_take(self.set_b, m)
        self.widen_rows(self.got_b, self.row_b, m)

        def send(s):
            c = lax.rem(self.chan + s, PER)
            self.copy_b(m, c, self.row, 2 * c + self.half).start()

        each(1, PER, send)
        self.own_b(m).start()

    def pass_b(self, m):
        def pass_on(s):
            c = lax.rem(self.chan + s, PER)
            source = 2 * c + self.half
            self.copy_b(m, c, source, source).wait_recv()
            self.hand(m, source).start()

        self.own_b(m).wait()
        self.hand(m, self.row).start()
        each(1, PER, pass_on)

    def take_b(self, m):
        each(0, PER, lambda c: self.hand(m, 2 * c + (1 - self.half)).wait_recv())

    def sent_b(self, m):
        each(
            1, PER,
            lambda s: self.copy_b(
                m, lax.rem(self.chan + s, PER), self.row, self.row
            ).wait_send(),
        )
        each(0, PER, lambda c: self.hand(m, 2 * c + self.half).wait_send())

    def pair_a(self, m, s, source):
        if self.outgoing:
            return self.row_a.at[m, s], self.left.at[m, lax.rem(source, 8)], 2 * s + source // 8
        there = self.left.at[m, source // 8, :, lax.rem(source, 8)]
        return self.row_a.at[m, s // 2, lax.rem(s, 2)], there, s

    def each_a(self, m, remote_step, own_step):
        def step(s):
            src, dst, peer = self.pair_a(m, s, self.row)

            @pl.when(peer != self.row)
            def _():
                remote_step(
                    remote(
                        src, dst, self.sa2.at[m, s], self.ra2.at[m, self.row], "row", peer
                    )
                )

            if own_step is not None:

                @pl.when(peer == self.row)
                def _():
                    own_step(pltpu.make_async_copy(src, dst, self.ra2.at[m, self.row]))

        each(0, 8 if self.outgoing else 16, step)

    def spread_a(self, m):
        self.col_take(self.set_a, m)
        if self.outgoing:
            self.widen_rows(self.got_a, self.row_a, m)
        else:
            self.widen_lanes(self.got_a, self.row_a, m)
        self.each_a(m, lambda copy: copy.start(), lambda copy: copy.start())

    def take_a(self, m):
        def step(s):
            source = self.half * 8 + s if self.outgoing else s
            src, dst, _ = self.pair_a(m, 0, source)

            @pl.when(source != self.row)
            def _():
                remote(
                    src, dst, self.sa2.at[m, 0], self.ra2.at[m, source], "row", source
                ).wait_recv()

            @pl.when(source == self.row)
            def _():
                pltpu.make_async_copy(src, dst, self.ra2.at[m, source]).wait()

        each(0, 8 if self.outgoing else 16, step)

    def sent_a(self, m):
        self.each_a(m, lambda copy: copy.wait_send(), None)

    def copy_p(self, m, s, peer, slot):
        return remote(
            self.send_p.at[m, s], self.got_p.at[m, slot], self.s3.at[m, s],
            self.r3.at[m, slot], "row", peer,
        )

    def own_p(self, m):
        return pltpu.make_async_copy(
            self.send_p.at[m, lax.rem(self.row, 8)], self.got_p.at[m, self.chan],
            self.r3.at[m, self.chan],
        )

    def multiply(self, m):
        right = self.right[...].reshape(N, N)
        if self.outgoing:
            made = lax.dot_general(
                self.left[m].reshape(128, N), right, NT, preferred_element_type=F32
            )
        else:
            made = lax.dot_general(
                self.left[m].reshape(N, 128), right, TN, preferred_element_type=F32
            )
        self.send_p[m] = made.astype(BF16).reshape(8, 16, N)

        def send(s):
            peer = self.half * 8 + s

            @pl.when(peer != self.row)
            def _():
                self.copy_p(m, s, peer, self.chan).start()

        each(0, 8, send)

        @pl.when(self.row // 8 == self.half)
        def _():
            self.own_p(m).start()

    def sent_p(self, m):
        def step(s):
            peer = self.half * 8 + s

            @pl.when(peer != self.row)
            def _():
                self.copy_p(m, s, peer, self.chan).wait_send()

        each(0, 8, step)

    def back(self, m):
        def take(c):
            source = 2 * c + self.row // 8

            @pl.when(source != self.row)
            def _():
                self.copy_p(m, 0, source, c).wait_recv()

            @pl.when(source == self.row)
            def _():
                self.own_p(m).wait()

        each(0, PER, take)
        for c in range(PER):
            for tile in range(2 * TH):
                self.wide[tile, pl.ds(c, 16, stride=8), :] = self.got_p[
                    m, c, :, 128 * tile : 128 * tile + 128
                ].astype(F32)

        def side(u):
            for t in range(TH):
                v = [
                    jnp.concatenate(
                        [
                            self.wide[u * TH + t, e * 64 + il * 8 : e * 64 + il * 8 + 8]
                            for e in range(2)
                        ],
                        axis=0,
                    )
                    for il in range(8)
                ]
                for q, w in enumerate(block_transpose(v)):
                    self.send_o[m, 8 * u + q, :, :, 128 * t : 128 * t + 128] = w.reshape(
                        2, PER, 128
                    ).astype(BF16)

        each(0, 2, side)
        self.col_start(self.set_o, m)

    def finish(self, m, e):
        ih = 2 * m + e
        x = self.got_o[m, :, e].astype(F32).reshape(C, LANES)
        x = normalize(x, 0) * jnp.concatenate([self.scale_t[...]] * TH, axis=1)
        change = lax.dot_general(
            x.astype(BF16), self.final[...], TN, preferred_element_type=F32
        )
        change = change * self.gate[lines_of(ih), :]
        return (self.field[lines_of(ih), :].astype(F32) + change).astype(BF16)

    def middle(self):
        self.spread_b(0)
        self.spread_b(1)
        self.pass_b(0)
        self.spread_b(2)
        self.pass_b(1)
        self.spread_a(0)
        self.pass_b(2)
        self.spread_a(1)
        for m in range(TH):
            self.take_b(m)
        self.take_a(0)
        self.multiply(0)
        self.spread_a(2)
        self.take_a(1)
        self.multiply(1)
        self.back(0)
        self.take_a(2)
        self.multiply(2)
        self.back(1)
        self.back(2)

    def sent(self):
        for m in range(TH):
            self.col_sent(self.set_b, m)
            self.col_sent(self.set_a, m)
            self.sent_b(m)
            self.sent_a(m)
            self.sent_p(m)
            self.col_sent(self.set_o, m)


def kernel(z_ref, n1, m1, s1, f1, n2, m2, s2, f2, out_ref, wide, *refs):
    count = len(refs) // 2
    one = Update(True, wide, n1, m1, s1, f1, refs[:count])
    two = Update(False, wide, n2, m2, s2, f2, refs[count:])
    barrier = pltpu.get_barrier_semaphore()

    def greet(s):
        for axis, place in (("row", one.row), ("col", one.col)):
            pl.semaphore_signal(
                barrier, inc=1, device_id={axis: lax.rem(place + s, 16)}, device_id_type=MESH
            )

    each(1, 16, greet)
    one.ready()
    for m in range(TH):

        def load(e):
            ih = 2 * m + e
            lines = pl.ds(pl.multiple_of(ih * 8, 8), 8)
            one.field[lines_of(ih), :] = jnp.concatenate(
                [z_ref[lines, 16 * t : 16 * t + 16, :].reshape(128, C) for t in range(TH)],
                axis=0,
            )
            one.prepare(ih)

        each(0, 2, load)
        one.make_b(m)
        if m == 0:
            pl.semaphore_wait(barrier, 30)
        one.col_start(one.set_b, m)
    for m in range(TH):
        one.make_a(m)
        one.col_start(one.set_a, m)
    each(0, IH, one.gating)
    two.ready()
    one.middle()
    for m in range(TH):
        one.col_take(one.set_o, m)

        def pass_on(e):
            ih = 2 * m + e
            two.field[lines_of(ih), :] = one.finish(m, e)
            two.prepare(ih)

        each(0, 2, pass_on)
        two.make_b(m)
        two.col_start(two.set_b, m)
    for m in range(TH):
        two.make_a(m)
    for m in range(TH):
        two.col_start(two.set_a, m)
    each(0, IH, two.gating)
    two.middle()
    for m in range(TH):
        two.col_take(two.set_o, m)

        def close(e):
            made = two.finish(m, e)
            lines = pl.ds(pl.multiple_of((2 * m + e) * 8, 8), 8)
            for t in range(TH):
                out_ref[lines, 16 * t : 16 * t + 16, :] = made[
                    128 * t : 128 * t + 128
                ].reshape(8, 16, C)

        each(0, 2, close)
    one.sent()
    two.sent()


def body(state, n1, m1, s1, f1, n2, m2, s2, f2):
    return pl.pallas_call(
        kernel,
        out_shape=jax.ShapeDtypeStruct(state.shape, state.dtype),
        scratch_shapes=[pltpu.VMEM((2 * TH, 16 * PER, 128), F32)]
        + buffers(True)
        + buffers(False),
        name="triangle",
        compiler_params=pltpu.CompilerParams(collective_id=1, has_side_effects=True),
    )(
        state,
        n1.reshape(1, C), m1, s1.reshape(1, C), f1,
        n2.reshape(1, C), m2, s2.reshape(1, C), f2,
    )


def solution(mesh):
    placed = (P("row", "col", None), P(), P(), P(), P(), P(), P(), P(), P())
    return jax.shard_map(
        body, mesh=mesh, in_specs=placed, out_specs=P("row", "col", None), check_vma=False
    )
```

```python
import jax
import jax.numpy as jnp
from jax import lax
from jax.experimental import pallas as pl
from jax.experimental.pallas import tpu as pltpu
from jax.sharding import PartitionSpec as P

MESH = pl.DeviceIdType.MESH
N_ROW, N_COL, T, C = 16, 16, 48, 128
PER = C // N_COL
N = N_ROW * T
IH, TH = T // 8, T // 16
LANES = TH * 128
F32, BF16 = jnp.float32, jnp.bfloat16
NT = (((1,), (1,)), ((), ()))
TN = (((0,), (0,)), ((), ()))


def normalize(x, axis):
    center = jnp.mean(x, axis=axis, keepdims=True)
    spread = jnp.mean((x - center) ** 2, axis=axis, keepdims=True)
    return (x - center) * lax.rsqrt(spread + 1e-05)


def block_transpose(v):
    block = lax.broadcasted_iota(jnp.int32, v[0].shape, 1) // 16
    for step in (1, 2, 4):
        low = (block & step) == 0
        out = list(v)
        for a in range(8):
            if a & step == 0:
                x, y = v[a], v[a + step]
                out[a] = jnp.where(low, x, pltpu.roll(y, 16 * step, 1))
                out[a + step] = jnp.where(low, pltpu.roll(x, 128 - 16 * step, 1), y)
        v = out
    return v


def each(first, last, body):
    def step(s, carry):
        body(s)
        return carry

    lax.fori_loop(first, last, step, 0)


def lines_of(ih):
    return pl.ds(pl.multiple_of(ih * LANES, LANES), LANES)


def remote(src, dst, send, recv, axis, peer):
    return pltpu.make_async_remote_copy(
        src_ref=src, dst_ref=dst, send_sem=send, recv_sem=recv,
        device_id={axis: peer}, device_id_type=MESH,
    )


def arrived(ref, sem):
    pltpu.make_async_copy(ref, ref, sem).wait()


BUFFERS = (
    "wt", "normed", "gate", "scale_t", "field",
    "send_b", "got_b", "send_a", "got_a",
    "row_b", "right", "row_a", "left", "send_p", "got_p", "send_o", "got_o",
    "sb1", "rb1", "sa1", "ra1", "sb2", "rb2", "sf", "rf", "sa2", "ra2", "s3", "r3", "s4", "r4",
)


def buffers(outgoing):
    vm, dma = pltpu.VMEM, pltpu.SemaphoreType.DMA
    rows = (TH, N_COL, 2, PER, LANES)
    first = rows if outgoing else (TH, N_COL, IH, PER, 128)
    return [
        vm((5 * C, C), BF16), vm((T * T, C), BF16), vm((T * T, C), F32), vm((C, C), F32),
        vm((T * T, C), BF16),
        vm(rows, BF16), vm(rows, BF16), vm(first, BF16), vm(first, BF16),
        vm((TH, PER, 16, N), BF16), vm((2, TH, 4, 2, 16, N), BF16),
        vm((TH, PER, 16, N) if outgoing else (TH, N_ROW, TH, 16, 128), BF16),
        vm((TH, 8, 16, N) if outgoing else (TH, 2, TH, 8, 16, 128), BF16),
        vm((TH, 8, 16, N), BF16), vm((TH, PER, 16, N), BF16),
        vm(rows, BF16), vm(rows, BF16),
    ] + [dma((TH,))] * 14


class Update:
    def __init__(self, outgoing, wide, gain, weights, scale, final, refs):
        self.outgoing, self.wide = outgoing, wide
        self.gain, self.weights, self.scale, self.final = gain, weights, scale, final
        self.__dict__.update(zip(BUFFERS, refs))
        self.row, self.col = lax.axis_index("row"), lax.axis_index("col")
        self.chan, self.half = self.row // 2, self.row % 2

    def ready(self):
        self.wt[...] = jnp.transpose(self.weights[...].astype(F32)).astype(BF16)
        self.scale_t[...] = jnp.transpose(jnp.broadcast_to(self.scale[...], (C, C)))

    def prepare(self, ih):
        x = self.field[lines_of(ih), :].astype(F32)
        self.normed[lines_of(ih), :] = (normalize(x, 1) * self.gain[...]).astype(BF16)

    def project(self, array, ih):
        x, base = self.normed[lines_of(ih), :], 2 * C * array
        g = lax.dot_general(self.wt[base : base + C, :], x, NT, preferred_element_type=F32)
        v = lax.dot_general(
            self.wt[base + C : base + 2 * C, :], x, NT, preferred_element_type=F32
        )
        return jax.nn.sigmoid(g) * v

    def make_b(self, m):
        for e in range(2):
            made = self.project(1, 2 * m + e)
            self.send_b[m, :, e] = made.reshape(N_COL, PER, LANES).astype(BF16)

    def make_a(self, m):
        for e in range(2):
            made = self.project(0, 2 * m + e)
            if self.outgoing:
                self.send_a[m, :, e] = made.reshape(N_COL, PER, LANES).astype(BF16)
            else:
                for t in range(TH):
                    piece = made[:, 128 * t : 128 * t + 128].reshape(N_COL, PER, 128)
                    self.send_a[t, :, 2 * m + e] = piece.astype(BF16)

    def gating(self, ih):
        self.gate[lines_of(ih), :] = jax.nn.sigmoid(
            jnp.dot(
                self.normed[lines_of(ih), :], self.weights[:, 4 * C :],
                preferred_element_type=F32,
            )
        )

    def col_start(self, sets, m):
        src, dst, send, recv = sets

        def start(s):
            peer = lax.rem(self.col + s, N_COL)
            remote(
                src.at[m, peer], dst.at[m, self.col], send.at[m], recv.at[m], "col", peer
            ).start()

        each(1, N_COL, start)
        pltpu.make_async_copy(src.at[m, self.col], dst.at[m, self.col], recv.at[m]).start()

    def col_take(self, sets, m):
        arrived(sets[1].at[m], sets[3].at[m])

    def col_sent(self, sets, m):
        arrived(sets[0].at[m, 0 : N_COL - 1], sets[2].at[m])

    @property
    def set_b(self):
        return self.send_b, self.got_b, self.sb1, self.rb1

    @property
    def set_a(self):
        return self.send_a, self.got_a, self.sa1, self.ra1

    @property
    def set_o(self):
        return self.send_o, self.got_o, self.s4, self.r4

    def widen_rows(self, got, out, m):
        def side(u):
            for t in range(TH):
                v = [
                    got[m, 8 * u + q, :, :, 128 * t : 128 * t + 128]
                    .astype(F32)
                    .reshape(2 * PER, 128)
                    for q in range(8)
                ]
                for il, w in enumerate(block_transpose(v)):
                    for e in range(2):
                        self.wide[
                            u * TH + t, e * 64 + il * 8 : e * 64 + il * 8 + 8
                        ] = w[e * 8 : e * 8 + 8]

        each(0, 2, side)
        for c in range(PER):
            for tile in range(2 * TH):
                out[m, c, :, 128 * tile : 128 * tile + 128] = self.wide[
                    tile, pl.ds(c, 16, stride=8), :
                ].astype(BF16)

    def widen_lanes(self, got, out, t):
        def side(u):
            v = [
                got[t, 8 * u + q].astype(F32).reshape(IH * PER, 128) for q in range(8)
            ]
            for il, w in enumerate(block_transpose(v)):
                for ih in range(IH):
                    third, e = ih // 2, ih % 2
                    self.wide[
                        u * TH + third, e * 64 + il * 8 : e * 64 + il * 8 + 8
                    ] = w[ih * 8 : ih * 8 + 8]

        each(0, 2, side)
        for c in range(PER):
            for u in range(2):
                for third in range(TH):
                    out[t, 2 * c + u, third] = self.wide[
                        u * TH + third, pl.ds(c, 16, stride=8), :
                    ].astype(BF16)

    def place_b(self, m):
        return self.right.at[self.row // 8, m, lax.rem(self.row, 8) // 2, self.half]

    def spread_b(self, m):
        self.col_take(self.set_b, m)
        self.widen_rows(self.got_b, self.row_b, m)

        def send(s):
            c = lax.rem(self.chan + s, PER)
            remote(
                self.row_b.at[m, c], self.place_b(m), self.sb2.at[m], self.rb2.at[m],
                "row", 2 * c + self.half,
            ).start()

        each(1, PER, send)
        pltpu.make_async_copy(
            self.row_b.at[m, self.chan], self.place_b(m), self.rb2.at[m]
        ).start()

    def hand(self, m):
        there = self.right.at[:, m, :, self.half]
        return remote(
            there, there, self.sf.at[m], self.rf.at[m], "row", self.chan * 2 + (1 - self.half)
        )

    def pass_b(self, m):
        arrived(self.right.at[:, m, :, self.half], self.rb2.at[m])
        self.hand(m).start()

    def take_b(self, m):
        arrived(self.right.at[:, m, :, 1 - self.half], self.rf.at[m])

    def sent_b(self, m):
        arrived(self.row_b.at[m, 0 : PER - 1], self.sb2.at[m])
        self.hand(m).wait_send()

    def start_a(self, m):
        if self.outgoing:
            there = self.left.at[m, lax.rem(self.row, 8)]
        else:
            there = self.left.at[m, self.row // 8, :, lax.rem(self.row, 8)]

        def step(s):
            peer = 2 * s + self.row // 8 if self.outgoing else s
            src = self.row_a.at[m, s]

            @pl.when(peer != self.row)
            def _():
                remote(src, there, self.sa2.at[m], self.ra2.at[m], "row", peer).start()

            @pl.when(peer == self.row)
            def _():
                pltpu.make_async_copy(src, there, self.ra2.at[m]).start()

        each(0, 8 if self.outgoing else 16, step)

    def sent_some(self, ref, m, sem):
        mine = self.row // 8 == self.half

        @pl.when(mine)
        def _():
            arrived(ref.at[m, 0:7], sem.at[m])

        @pl.when(jnp.logical_not(mine))
        def _():
            arrived(ref.at[m], sem.at[m])

    def spread_a(self, m):
        self.col_take(self.set_a, m)
        if self.outgoing:
            self.widen_rows(self.got_a, self.row_a, m)
        else:
            self.widen_lanes(self.got_a, self.row_a, m)
        self.start_a(m)

    def take_a(self, m):
        arrived(self.left.at[m], self.ra2.at[m])

    def sent_a(self, m):
        if self.outgoing:
            self.sent_some(self.row_a, m, self.sa2)
        else:
            arrived(self.row_a.at[m, 0 : N_ROW - 1], self.sa2.at[m])

    def multiply(self, m):
        right = self.right[...].reshape(N, N)
        if self.outgoing:
            made = lax.dot_general(
                self.left[m].reshape(128, N), right, NT, preferred_element_type=F32
            )
        else:
            made = lax.dot_general(
                self.left[m].reshape(N, 128), right, TN, preferred_element_type=F32
            )
        self.send_p[m] = made.astype(BF16).reshape(8, 16, N)

        def send(s):
            peer = self.half * 8 + s

            src, there = self.send_p.at[m, s], self.got_p.at[m, self.chan]

            @pl.when(peer != self.row)
            def _():
                remote(src, there, self.s3.at[m], self.r3.at[m], "row", peer).start()

            @pl.when(peer == self.row)
            def _():
                pltpu.make_async_copy(src, there, self.r3.at[m]).start()

        each(0, 8, send)

    def sent_p(self, m):
        self.sent_some(self.send_p, m, self.s3)

    def back(self, m):
        arrived(self.got_p.at[m], self.r3.at[m])
        for c in range(PER):
            for tile in range(2 * TH):
                self.wide[tile, pl.ds(c, 16, stride=8), :] = self.got_p[
                    m, c, :, 128 * tile : 128 * tile + 128
                ].astype(F32)

        def side(u):
            for t in range(TH):
                v = [
                    jnp.concatenate(
                        [
                            self.wide[u * TH + t, e * 64 + il * 8 : e * 64 + il * 8 + 8]
                            for e in range(2)
                        ],
                        axis=0,
                    )
                    for il in range(8)
                ]
                for q, w in enumerate(block_transpose(v)):
                    self.send_o[m, 8 * u + q, :, :, 128 * t : 128 * t + 128] = w.reshape(
                        2, PER, 128
                    ).astype(BF16)

        each(0, 2, side)
        self.col_start(self.set_o, m)

    def finish(self, m, e):
        ih = 2 * m + e
        x = self.got_o[m, :, e].astype(F32).reshape(C, LANES)
        x = normalize(x, 0) * jnp.concatenate([self.scale_t[...]] * TH, axis=1)
        change = lax.dot_general(
            x.astype(BF16), self.final[...], TN, preferred_element_type=F32
        )
        change = change * self.gate[lines_of(ih), :]
        return (self.field[lines_of(ih), :].astype(F32) + change).astype(BF16)

    def middle(self):
        self.spread_b(0)
        self.spread_b(1)
        self.pass_b(0)
        self.spread_b(2)
        self.pass_b(1)
        self.spread_a(0)
        self.pass_b(2)
        self.spread_a(1)
        for m in range(TH):
            self.take_b(m)
        self.take_a(0)
        self.multiply(0)
        self.spread_a(2)
        self.take_a(1)
        self.multiply(1)
        self.back(0)
        self.take_a(2)
        self.multiply(2)
        self.back(1)
        self.back(2)

    def sent(self):
        for m in range(TH):
            self.col_sent(self.set_b, m)
            self.col_sent(self.set_a, m)
            self.sent_b(m)
            self.sent_a(m)
            self.sent_p(m)
            self.col_sent(self.set_o, m)


def kernel(z_ref, n1, m1, s1, f1, n2, m2, s2, f2, out_ref, wide, *refs):
    count = len(refs) // 2
    one = Update(True, wide, n1, m1, s1, f1, refs[:count])
    two = Update(False, wide, n2, m2, s2, f2, refs[count:])
    barrier = pltpu.get_barrier_semaphore()

    def greet(s):
        for axis, place in (("row", one.row), ("col", one.col)):
            pl.semaphore_signal(
                barrier, inc=1, device_id={axis: lax.rem(place + s, 16)}, device_id_type=MESH
            )

    each(1, 16, greet)
    one.ready()
    for m in range(TH):

        def load(e):
            ih = 2 * m + e
            lines = pl.ds(pl.multiple_of(ih * 8, 8), 8)
            one.field[lines_of(ih), :] = jnp.concatenate(
                [z_ref[lines, 16 * t : 16 * t + 16, :].reshape(128, C) for t in range(TH)],
                axis=0,
            )
            one.prepare(ih)

        each(0, 2, load)
        one.make_b(m)
        if m == 0:
            pl.semaphore_wait(barrier, 30)
        one.col_start(one.set_b, m)
    for m in range(TH):
        one.make_a(m)
        one.col_start(one.set_a, m)
    each(0, IH, one.gating)
    two.ready()
    one.middle()
    for m in range(TH):
        one.col_take(one.set_o, m)

        def pass_on(e):
            ih = 2 * m + e
            two.field[lines_of(ih), :] = one.finish(m, e)
            two.prepare(ih)

        each(0, 2, pass_on)
        two.make_b(m)
        two.col_start(two.set_b, m)
    for m in range(TH):
        two.make_a(m)
    for m in range(TH):
        two.col_start(two.set_a, m)
    each(0, IH, two.gating)
    two.middle()
    one.sent()
    for m in range(TH):
        two.col_take(two.set_o, m)

        def close(e):
            made = two.finish(m, e)
            lines = pl.ds(pl.multiple_of((2 * m + e) * 8, 8), 8)
            for t in range(TH):
                out_ref[lines, 16 * t : 16 * t + 16, :] = made[
                    128 * t : 128 * t + 128
                ].reshape(8, 16, C)

        each(0, 2, close)
    two.sent()


def body(state, n1, m1, s1, f1, n2, m2, s2, f2):
    return pl.pallas_call(
        kernel,
        out_shape=jax.ShapeDtypeStruct(state.shape, state.dtype),
        scratch_shapes=[pltpu.VMEM((2 * TH, 16 * PER, 128), F32)]
        + buffers(True)
        + buffers(False),
        name="triangle",
        compiler_params=pltpu.CompilerParams(collective_id=1, has_side_effects=True),
    )(
        state,
        n1.reshape(1, C), m1, s1.reshape(1, C), f1,
        n2.reshape(1, C), m2, s2.reshape(1, C), f2,
    )


def solution(mesh):
    placed = (P("row", "col", None), P(), P(), P(), P(), P(), P(), P(), P())
    return jax.shard_map(
        body, mesh=mesh, in_specs=placed, out_specs=P("row", "col", None), check_vma=False
    )
```

```python
import jax
import jax.numpy as jnp
from jax import lax
from jax.experimental import pallas as pl
from jax.experimental.pallas import tpu as pltpu
from jax.sharding import PartitionSpec as P

MESH = pl.DeviceIdType.MESH
N_ROW, N_COL, T, C = 16, 16, 48, 128
PER = C // N_COL
N = N_ROW * T
IH, TH = T // 8, T // 16
LANES = TH * 128
F32, BF16 = jnp.float32, jnp.bfloat16
NT = (((1,), (1,)), ((), ()))
TN = (((0,), (0,)), ((), ()))


def normalize(x, axis):
    center = jnp.mean(x, axis=axis, keepdims=True)
    spread = jnp.mean((x - center) ** 2, axis=axis, keepdims=True)
    return (x - center) * lax.rsqrt(spread + 1e-05)


def block_transpose(v):
    block = lax.broadcasted_iota(jnp.int32, v[0].shape, 1) // 16
    for step in (1, 2, 4):
        low = (block & step) == 0
        out = list(v)
        for a in range(8):
            if a & step == 0:
                x, y = v[a], v[a + step]
                out[a] = jnp.where(low, x, pltpu.roll(y, 16 * step, 1))
                out[a + step] = jnp.where(low, pltpu.roll(x, 128 - 16 * step, 1), y)
        v = out
    return v


def each(first, last, body):
    def step(s, carry):
        body(s)
        return carry

    lax.fori_loop(first, last, step, 0)


def lines_of(ih):
    return pl.ds(pl.multiple_of(ih * LANES, LANES), LANES)


def remote(src, dst, send, recv, axis, peer):
    return pltpu.make_async_remote_copy(
        src_ref=src, dst_ref=dst, send_sem=send, recv_sem=recv,
        device_id={axis: peer}, device_id_type=MESH,
    )


def arrived(ref, sem):
    pltpu.make_async_copy(ref, ref, sem).wait()


BUFFERS = (
    "wt", "normed", "gate", "scale_t", "field",
    "send_b", "got_b", "send_a", "got_a",
    "row_b", "right", "row_a", "left", "send_p", "got_p", "send_o", "got_o",
    "sb1", "rb1", "sa1", "ra1", "sb2", "rb2", "sf", "rf", "sa2", "ra2", "s3", "r3", "s4", "r4",
)


def buffers(outgoing):
    vm, dma = pltpu.VMEM, pltpu.SemaphoreType.DMA
    rows = (TH, N_COL, 2, PER, LANES)
    first = rows if outgoing else (TH, N_COL, IH, PER, 128)
    return [
        vm((5 * C, C), BF16), vm((T * T, C), BF16), vm((T * T, C), F32), vm((C, C), F32),
        vm((T * T, C), BF16),
        vm(rows, BF16), vm(rows, BF16), vm(first, BF16), vm(first, BF16),
        vm((TH, PER, 16, N), BF16), vm((2, TH, 4, 2, 16, N), BF16),
        vm((TH, PER, 16, N) if outgoing else (TH, N_ROW, TH, 16, 128), BF16),
        vm((TH, 8, 16, N) if outgoing else (TH, 2, TH, 8, 16, 128), BF16),
        vm((TH, 8, 16, N), BF16), vm((TH, PER, 16, N), BF16),
        vm(rows, BF16), vm(rows, BF16),
    ] + [dma((TH,))] * 14


class Update:
    def __init__(self, outgoing, wide, gain, weights, scale, final, refs):
        self.outgoing, self.wide = outgoing, wide
        self.gain, self.weights, self.scale, self.final = gain, weights, scale, final
        self.__dict__.update(zip(BUFFERS, refs))
        self.row, self.col = lax.axis_index("row"), lax.axis_index("col")
        self.chan, self.half = self.row // 2, self.row % 2

    def ready(self):
        self.wt[...] = jnp.transpose(self.weights[...].astype(F32)).astype(BF16)
        self.scale_t[...] = jnp.transpose(jnp.broadcast_to(self.scale[...], (C, C)))

    def prepare(self, ih):
        x = self.field[lines_of(ih), :].astype(F32)
        self.normed[lines_of(ih), :] = (normalize(x, 1) * self.gain[...]).astype(BF16)

    def project(self, array, ih):
        x, base = self.normed[lines_of(ih), :], 2 * C * array
        g = lax.dot_general(self.wt[base : base + C, :], x, NT, preferred_element_type=F32)
        v = lax.dot_general(
            self.wt[base + C : base + 2 * C, :], x, NT, preferred_element_type=F32
        )
        return jax.nn.sigmoid(g) * v

    def make_b(self, m):
        for e in range(2):
            made = self.project(1, 2 * m + e)
            self.send_b[m, :, e] = made.reshape(N_COL, PER, LANES).astype(BF16)

    def make_a(self, m):
        for e in range(2):
            made = self.project(0, 2 * m + e)
            if self.outgoing:
                self.send_a[m, :, e] = made.reshape(N_COL, PER, LANES).astype(BF16)
            else:
                for t in range(TH):
                    piece = made[:, 128 * t : 128 * t + 128].reshape(N_COL, PER, 128)
                    self.send_a[t, :, 2 * m + e] = piece.astype(BF16)

    def gating(self, ih):
        self.gate[lines_of(ih), :] = jax.nn.sigmoid(
            jnp.dot(
                self.normed[lines_of(ih), :], self.weights[:, 4 * C :],
                preferred_element_type=F32,
            )
        )

    def col_start(self, sets, m):
        src, dst, send, recv = sets

        def start(s):
            peer = lax.rem(self.col + s, N_COL)
            remote(
                src.at[m, peer], dst.at[m, self.col], send.at[m], recv.at[m], "col", peer
            ).start()

        each(1, N_COL, start)
        pltpu.make_async_copy(src.at[m, self.col], dst.at[m, self.col], recv.at[m]).start()

    def col_take(self, sets, m):
        arrived(sets[1].at[m], sets[3].at[m])

    def col_sent(self, sets, m):
        arrived(sets[0].at[m, 0 : N_COL - 1], sets[2].at[m])

    @property
    def set_b(self):
        return self.send_b, self.got_b, self.sb1, self.rb1

    @property
    def set_a(self):
        return self.send_a, self.got_a, self.sa1, self.ra1

    @property
    def set_o(self):
        return self.send_o, self.got_o, self.s4, self.r4

    def widen_rows(self, got, out, m):
        def side(u):
            for t in range(TH):
                v = [
                    got[m, 8 * u + q, :, :, 128 * t : 128 * t + 128]
                    .astype(F32)
                    .reshape(2 * PER, 128)
                    for q in range(8)
                ]
                for il, w in enumerate(block_transpose(v)):
                    for e in range(2):
                        self.wide[
                            u * TH + t, e * 64 + il * 8 : e * 64 + il * 8 + 8
                        ] = w[e * 8 : e * 8 + 8]

        each(0, 2, side)
        for c in range(PER):
            for tile in range(2 * TH):
                out[m, c, :, 128 * tile : 128 * tile + 128] = self.wide[
                    tile, pl.ds(c, 16, stride=8), :
                ].astype(BF16)

    def widen_lanes(self, got, out, t):
        def side(u):
            v = [
                got[t, 8 * u + q].astype(F32).reshape(IH * PER, 128) for q in range(8)
            ]
            for il, w in enumerate(block_transpose(v)):
                for ih in range(IH):
                    third, e = ih // 2, ih % 2
                    self.wide[
                        u * TH + third, e * 64 + il * 8 : e * 64 + il * 8 + 8
                    ] = w[ih * 8 : ih * 8 + 8]

        each(0, 2, side)
        for c in range(PER):
            for u in range(2):
                for third in range(TH):
                    out[t, 2 * c + u, third] = self.wide[
                        u * TH + third, pl.ds(c, 16, stride=8), :
                    ].astype(BF16)

    def place_b(self, m):
        return self.right.at[self.row // 8, m, lax.rem(self.row, 8) // 2, self.half]

    def spread_b(self, m):
        self.col_take(self.set_b, m)
        self.widen_rows(self.got_b, self.row_b, m)

        def send(s):
            c = lax.rem(self.chan + s, PER)
            remote(
                self.row_b.at[m, c], self.place_b(m), self.sb2.at[m], self.rb2.at[m],
                "row", 2 * c + self.half,
            ).start()

        each(1, PER, send)
        pltpu.make_async_copy(
            self.row_b.at[m, self.chan], self.place_b(m), self.rb2.at[m]
        ).start()

    def hand(self, m):
        there = self.right.at[:, m, :, self.half]
        return remote(
            there, there, self.sf.at[m], self.rf.at[m], "row", self.chan * 2 + (1 - self.half)
        )

    def pass_b(self, m):
        arrived(self.right.at[:, m, :, self.half], self.rb2.at[m])
        self.hand(m).start()

    def take_b(self, m):
        arrived(self.right.at[:, m, :, 1 - self.half], self.rf.at[m])

    def sent_b(self, m):
        arrived(self.row_b.at[m, 0 : PER - 1], self.sb2.at[m])
        self.hand(m).wait_send()

    def start_a(self, m):
        if self.outgoing:
            there = self.left.at[m, lax.rem(self.row, 8)]
        else:
            there = self.left.at[m, self.row // 8, :, lax.rem(self.row, 8)]

        def step(s):
            peer = 2 * s + self.row // 8 if self.outgoing else s
            src = self.row_a.at[m, s]

            @pl.when(peer != self.row)
            def _():
                remote(src, there, self.sa2.at[m], self.ra2.at[m], "row", peer).start()

            @pl.when(peer == self.row)
            def _():
                pltpu.make_async_copy(src, there, self.ra2.at[m]).start()

        each(0, 8 if self.outgoing else 16, step)

    def sent_some(self, ref, m, sem):
        mine = self.row // 8 == self.half

        @pl.when(mine)
        def _():
            arrived(ref.at[m, 0:7], sem.at[m])

        @pl.when(jnp.logical_not(mine))
        def _():
            arrived(ref.at[m], sem.at[m])

    def spread_a(self, m):
        self.col_take(self.set_a, m)
        if self.outgoing:
            self.widen_rows(self.got_a, self.row_a, m)
        else:
            self.widen_lanes(self.got_a, self.row_a, m)
        self.start_a(m)

    def take_a(self, m):
        arrived(self.left.at[m], self.ra2.at[m])

    def sent_a(self, m):
        if self.outgoing:
            self.sent_some(self.row_a, m, self.sa2)
        else:
            arrived(self.row_a.at[m, 0 : N_ROW - 1], self.sa2.at[m])

    def multiply(self, m):
        right = self.right[...].reshape(N, N)
        if self.outgoing:
            made = lax.dot_general(
                self.left[m].reshape(128, N), right, NT, preferred_element_type=F32
            )
        else:
            made = lax.dot_general(
                self.left[m].reshape(N, 128), right, TN, preferred_element_type=F32
            )
        self.send_p[m] = made.astype(BF16).reshape(8, 16, N)

        def send(s):
            peer = self.half * 8 + s

            src, there = self.send_p.at[m, s], self.got_p.at[m, self.chan]

            @pl.when(peer != self.row)
            def _():
                remote(src, there, self.s3.at[m], self.r3.at[m], "row", peer).start()

            @pl.when(peer == self.row)
            def _():
                pltpu.make_async_copy(src, there, self.r3.at[m]).start()

        each(0, 8, send)

    def sent_p(self, m):
        self.sent_some(self.send_p, m, self.s3)

    def back(self, m):
        arrived(self.got_p.at[m], self.r3.at[m])
        for c in range(PER):
            for tile in range(2 * TH):
                self.wide[tile, pl.ds(c, 16, stride=8), :] = self.got_p[
                    m, c, :, 128 * tile : 128 * tile + 128
                ].astype(F32)

        def side(u):
            for t in range(TH):
                v = [
                    jnp.concatenate(
                        [
                            self.wide[u * TH + t, e * 64 + il * 8 : e * 64 + il * 8 + 8]
                            for e in range(2)
                        ],
                        axis=0,
                    )
                    for il in range(8)
                ]
                for q, w in enumerate(block_transpose(v)):
                    self.send_o[m, 8 * u + q, :, :, 128 * t : 128 * t + 128] = w.reshape(
                        2, PER, 128
                    ).astype(BF16)

        each(0, 2, side)
        self.col_start(self.set_o, m)

    def finish(self, m, e):
        ih = 2 * m + e
        x = self.got_o[m, :, e].astype(F32).reshape(C, LANES)
        x = normalize(x, 0) * jnp.concatenate([self.scale_t[...]] * TH, axis=1)
        change = lax.dot_general(
            x.astype(BF16), self.final[...], TN, preferred_element_type=F32
        )
        change = change * self.gate[lines_of(ih), :]
        return (self.field[lines_of(ih), :].astype(F32) + change).astype(BF16)

    def middle(self):
        self.spread_b(0)
        self.spread_b(1)
        self.pass_b(0)
        self.spread_b(2)
        self.pass_b(1)
        self.spread_a(0)
        self.pass_b(2)
        self.spread_a(1)
        for m in range(TH):
            self.take_b(m)
        self.take_a(0)
        self.multiply(0)
        self.spread_a(2)
        self.take_a(1)
        self.multiply(1)
        self.back(0)
        self.take_a(2)
        self.multiply(2)
        self.back(1)
        self.back(2)

    def sent(self):
        for m in range(TH):
            self.col_sent(self.set_b, m)
            self.col_sent(self.set_a, m)
            self.sent_b(m)
            self.sent_a(m)
            self.sent_p(m)
            self.col_sent(self.set_o, m)


def kernel(*refs):
    given, (out_ref, wide, loads), held, refs = refs[:9], refs[9:12], refs[12:21], refs[21:]
    z_ref, n1, m1, s1, f1, n2, m2, s2, f2 = held

    def load_of(i):
        return pltpu.make_async_copy(given[i], held[i], loads.at[i])

    count = len(refs) // 2
    one = Update(True, wide, n1, m1, s1, f1, refs[:count])
    two = Update(False, wide, n2, m2, s2, f2, refs[count:])
    barrier = pltpu.get_barrier_semaphore()

    def greet(s):
        for axis, place in (("row", one.row), ("col", one.col)):
            pl.semaphore_signal(
                barrier, inc=1, device_id={axis: lax.rem(place + s, 16)}, device_id_type=MESH
            )

    each(1, 16, greet)
    for i in (0, 2, 1, 3, 4, 5, 6, 7, 8):
        load_of(i).start()
    for i in (2, 3, 0, 1):
        load_of(i).wait()
    one.ready()
    for m in range(TH):

        def load(e):
            ih = 2 * m + e
            lines = pl.ds(pl.multiple_of(ih * 8, 8), 8)
            one.field[lines_of(ih), :] = jnp.concatenate(
                [z_ref[lines, 16 * t : 16 * t + 16, :].reshape(128, C) for t in range(TH)],
                axis=0,
            )
            one.prepare(ih)

        each(0, 2, load)
        one.make_b(m)
        if m == 0:
            pl.semaphore_wait(barrier, 30)
        one.col_start(one.set_b, m)
    for m in range(TH):
        one.make_a(m)
        one.col_start(one.set_a, m)
    each(0, IH, one.gating)
    for i in range(4, 9):
        load_of(i).wait()
    two.ready()
    one.middle()
    for m in range(TH):
        one.col_take(one.set_o, m)

        def pass_on(e):
            ih = 2 * m + e
            two.field[lines_of(ih), :] = one.finish(m, e)
            two.prepare(ih)

        each(0, 2, pass_on)
        two.make_b(m)
        two.col_start(two.set_b, m)
    for m in range(TH):
        two.make_a(m)
    for m in range(TH):
        two.col_start(two.set_a, m)
    each(0, IH, two.gating)
    two.middle()
    one.sent()
    for m in range(TH):
        two.col_take(two.set_o, m)

        def close(e):
            made = two.finish(m, e)
            lines = pl.ds(pl.multiple_of((2 * m + e) * 8, 8), 8)
            for t in range(TH):
                out_ref[lines, 16 * t : 16 * t + 16, :] = made[
                    128 * t : 128 * t + 128
                ].reshape(8, 16, C)

        each(0, 2, close)
    two.sent()


def body(state, n1, m1, s1, f1, n2, m2, s2, f2):
    return pl.pallas_call(
        kernel,
        out_shape=jax.ShapeDtypeStruct(state.shape, state.dtype),
        in_specs=[pl.BlockSpec(memory_space=pltpu.HBM)] * 9,
        scratch_shapes=[
            pltpu.VMEM((2 * TH, 16 * PER, 128), F32),
            pltpu.SemaphoreType.DMA((9,)),
            pltpu.VMEM(state.shape, BF16),
        ]
        + [
            pltpu.VMEM(shape, kind)
            for shape, kind in (
                ((1, C), F32), ((C, 5 * C), BF16), ((1, C), F32), ((C, C), BF16),
            )
        ]
        * 2
        + buffers(True)
        + buffers(False),
        name="triangle",
        compiler_params=pltpu.CompilerParams(collective_id=1, has_side_effects=True),
    )(
        state,
        n1.reshape(1, C), m1, s1.reshape(1, C), f1,
        n2.reshape(1, C), m2, s2.reshape(1, C), f2,
    )


def solution(mesh):
    placed = (P("row", "col", None), P(), P(), P(), P(), P(), P(), P(), P())
    return jax.shard_map(
        body, mesh=mesh, in_specs=placed, out_specs=P("row", "col", None), check_vma=False
    )
```
